128 devices in a mesh: col: 16 (over x, z_lo, core), row: 8 (over z_hi, y).
Axes of the slice: x: 4, y: 4, z: 4 (z_hi: 2, z_lo: 2; z = z_hi * 2 + z_lo), core: 2. Of those that a mesh axis runs over, the one named last changes fastest.
Arguments:
- features: bfloat16 [262144, 2048], P(('col', 'row')), may hold values from -6 to 6
- leaf_in: bfloat16 [262144, 128], P(('col', 'row')), may hold values from -0.1875 to 0.1875
- mix_in: bfloat16 [4, 256, 128, 256], P(None, ('col', 'row')), may hold values from -0.375 to 0.375
- mix_out: bfloat16 [4, 256, 128, 256], P(None, 'col'), may hold values from -0.375 to 0.375
- leaf_out: bfloat16 [262144, 128], P('col'), may hold values from -0.5 to 0.5
Outputs:
- result: bfloat16 [262144, 2048], P(('col', 'row'))
The draws below stay inside these ranges and needn't reach their ends.
All inputs are finite; a program needn't handle non-finite values.
Results may differ from the reference program's by a relative error of at most 0.023.
Values may be sent and summed in bfloat16 or wider, within the bound.
A program may use at most 128 MiB of HBM per device.

```python
import jax
import jax.numpy as jnp
from jax import lax

RANK = 128
LEAF_SIZE = 1024
RIGHT_SIDES = 2048
LEVELS_IN = 4
LEVELS_OUT = 4
LEAVES = 256
ORDER = 262144


def block_levels(own_key, shape, split, smallest, largest):
    gain = 1.0
    for axis_at, blocks in split:
        heights = jax.random.uniform(jax.random.fold_in(jax.random.fold_in(own_key, 6), axis_at), (blocks,), jnp.float32, smallest / len(split), largest / len(split))
        gain = gain * jnp.repeat(jnp.exp(heights), shape[axis_at] // blocks).reshape((-1,) + (1,) * (len(shape) - 1 - axis_at))
    return gain


def scatter_about(stream_key, shape, scale, bound, shards=(), kind=jnp.bfloat16):
    drawn = scale * jax.random.normal(stream_key, shape, jnp.float32)
    if shards:
        drawn = drawn * block_levels(stream_key, shape, shards, -0.22, 0.18)
    return jnp.clip(drawn, -bound, bound).astype(kind)


def setup_inputs(seed: int = 0) -> dict:
    key_of = jax.random.split(jax.random.key(seed), 6)
    return {
        "features": scatter_about(key_of[0], (ORDER, RIGHT_SIDES), 1.0, 6.0, ((0, 128),)),
        "leaf_in": scatter_about(key_of[1], (ORDER, RANK), LEAF_SIZE ** -0.5, 0.1875, ((0, 128),)),
        "mix_in": scatter_about(key_of[2], (LEVELS_IN, LEAVES, RANK, 2 * RANK), (2 * RANK) ** -0.5, 0.375, ((1, 128),)),
        "mix_out": scatter_about(key_of[3], (LEVELS_OUT, LEAVES, RANK, 2 * RANK), (2 * RANK) ** -0.5, 0.375, ((1, 16),)),
        "leaf_out": scatter_about(key_of[4], (ORDER, RANK), RANK ** -0.5, 0.5, ((0, 16),)),
    }


def partner_of(coeffs, level_bit):
    total_blocks = coeffs.shape[0]
    shaped = coeffs.reshape((total_blocks // (2 << level_bit), 2, 1 << level_bit) + coeffs.shape[1:])
    return jnp.flip(shaped, 1).reshape(coeffs.shape)


def forward_mix(weights, coeffs, level_bit):
    stacked = jnp.concatenate([coeffs, partner_of(coeffs, level_bit)], axis=1).astype(jnp.float32)
    return jnp.einsum('bkj,bjr->bkr', weights.astype(jnp.float32), stacked).astype(jnp.bfloat16)


def backward_mix(weights, gradient, level_bit):
    wide_weights = weights.astype(jnp.float32)
    wide_grad = gradient.astype(jnp.float32)
    direct = jnp.einsum('bjk,bjr->bkr', wide_weights[:, :, :RANK], wide_grad)
    crossed = jnp.einsum('bjk,bjr->bkr', wide_weights[:, :, RANK:], wide_grad).astype(jnp.bfloat16)
    return (direct + partner_of(crossed, level_bit).astype(jnp.float32)).astype(jnp.bfloat16)


def project(pieces):
    return jnp.dot(pieces[0].T, pieces[1], preferred_element_type=jnp.float32).astype(jnp.bfloat16)


def round_trip(pieces):
    images = jnp.dot(pieces[0], pieces[1], preferred_element_type=jnp.float32).astype(jnp.bfloat16)
    return jnp.dot(pieces[0].T, images, preferred_element_type=jnp.float32).astype(jnp.bfloat16)


def expand(pieces):
    return jnp.dot(pieces[0], pieces[1], preferred_element_type=jnp.float32).astype(jnp.bfloat16)


def reference(features, leaf_in, mix_in, mix_out, leaf_out):
    feature_blocks = features.reshape(LEAVES, LEAF_SIZE, RIGHT_SIDES)
    leaf_rows = leaf_in.reshape(LEAVES, LEAF_SIZE, RANK)
    out_rows = leaf_out.reshape(LEAVES, LEAF_SIZE, RANK)
    coeffs = lax.map(project, (leaf_rows, feature_blocks))
    for level_index in range(LEVELS_IN):
        coeffs = forward_mix(mix_in[level_index], coeffs, LEVELS_OUT + level_index)
    for level_index in range(LEVELS_OUT):
        coeffs = forward_mix(mix_out[level_index], coeffs, level_index)
    gradient = lax.map(round_trip, (out_rows, coeffs))
    for level_index in reversed(range(LEVELS_OUT)):
        gradient = backward_mix(mix_out[level_index], gradient, level_index)
    for level_index in reversed(range(LEVELS_IN)):
        gradient = backward_mix(mix_in[level_index], gradient, LEVELS_OUT + level_index)
    result = lax.map(expand, (leaf_rows, gradient))
    return result.reshape(ORDER, RIGHT_SIDES)
```

```python
import jax
import jax.numpy as jnp
from jax import lax
from jax.experimental import pallas as pl
from jax.experimental.pallas import tpu as pltpu
from jax.sharding import PartitionSpec as P

LEAF = 1024
RANK = 128
LANES = 128
MESH = pl.DeviceIdType.MESH
F32 = jnp.float32
BF16 = jnp.bfloat16
LEVELS = 4


def pairs_of(bit):
    return [b for b in range(16) if not b >> bit & 1]


def pair_matrix(top, bottom):
    swapped = jnp.concatenate([bottom[:, RANK:], bottom[:, :RANK]], axis=1)
    return jnp.concatenate([top, swapped], axis=0)


def column(x, zl, k):
    return x * 4 + zl * 2 + k


def operator_kernel(
    features, leaf_in, mix_in, mix_out, leaf_out, returned,
    feat, basis, basis_t, win, win_t, wout, wout_t, lout, gram,
    coeffs, xa, xb, xr, home,
    load_sem, w_send, w_recv, w_local, sib_send, sib_recv, send_sem, recv_sem, out_sem,
):
    col, row = lax.axis_index("col"), lax.axis_index("row")
    x, zl, k = col // 4, col // 2 % 2, col % 2
    zh, y = row // 4, row % 4
    x_hi, x_lo, y_hi, y_lo = x // 2, x % 2, y // 2, y % 2
    right, left = (x + 1) % 4, (x + 3) % 4

    feat_loads = [
        pltpu.make_async_copy(
            features.at[:, pl.ds(j * 512, 512)], feat.at[j], load_sem.at[j]
        )
        for j in range(4)
    ]
    basis_load = pltpu.make_async_copy(leaf_in, basis, load_sem.at[4])
    wout_load = pltpu.make_async_copy(mix_out, wout, load_sem.at[5])
    lout_load = pltpu.make_async_copy(leaf_out, lout, load_sem.at[6])
    own_load = pltpu.make_async_copy(mix_in.at[:, zl], win.at[col], load_sem.at[7])
    basis_load.start()
    for load in feat_loads:
        load.start()
    own_load.start()
    lout_load.start()
    wout_load.start()

    def relative(m):
        px = (x + m + 1) % 4
        pz = (zl + m + m // 4) % 2
        pk = (k + m // 2 + m // 8) % 2
        return px, pz, pk

    def spread_row(m, q):
        px, pz, pk = relative(m)
        py = (x_lo + q + px) % 2 * 2 + (x_hi + pk) % 2
        return column(px, pz, pk), k * 4 + py

    def gather_row(m, q):
        px = (y_lo + k) % 2 * 2 + (y_hi + q + x) % 2
        return column(px, m % 2, zh), m // 2

    barrier = pltpu.get_barrier_semaphore()

    def greet(m, carry):
        px, pz, pk = relative(m)
        pl.semaphore_signal(
            barrier, device_id={"col": column(px, pz, pk), "row": row}, device_id_type=MESH
        )
        for q in range(2):
            for c, r in (spread_row(m, q), gather_row(m, q)):
                pl.semaphore_signal(
                    barrier, device_id={"col": c, "row": r}, device_id_type=MESH
                )
        return carry

    lax.fori_loop(0, 16, greet, 0)
    pl.semaphore_wait(barrier, 80)

    def ship(src, dst, send, recv, c, r):
        here = jnp.logical_and(c == col, r == row)

        @pl.when(here)
        def _():
            pltpu.make_async_copy(src, dst, recv).start()

        @pl.when(jnp.logical_not(here))
        def _():
            pltpu.make_async_remote_copy(
                src_ref=src, dst_ref=dst, send_sem=send, recv_sem=recv,
                device_id={"col": c, "row": r}, device_id_type=MESH,
            ).start()

    def weights_to(src, slot, n, recv, c):
        return pltpu.make_async_remote_copy(
            src_ref=src, dst_ref=win.at[slot], send_sem=w_send.at[n], recv_sem=recv,
            device_id={"col": c}, device_id_type=MESH,
        )

    def arrived(slot, sem):
        pltpu.make_async_copy(win.at[slot], win.at[slot], sem).wait()

    def to_sibling(src, slot, n):
        copy = pltpu.make_async_remote_copy(
            src_ref=src, dst_ref=win.at[slot], send_sem=sib_send.at[n], recv_sem=sib_recv.at[n],
            device_id={"col": column(x, zl, 1 - k)}, device_id_type=MESH,
        )
        copy.start()
        return copy

    mine = mix_in.at[:, zl]
    partner = column(x, 1 - zl, k)
    w1 = weights_to(mix_in.at[:, 1 - zl], col, 0, w_recv.at[0], partner)
    w2 = [
        weights_to(mine, col, 1, w_recv.at[1 + zl], column(right, zl, k)),
        weights_to(mine, col, 2, w_recv.at[3 + zl], column(left, zl, k)),
    ]
    w1.start()
    w2[0].start()
    w2[1].start()
    siblings = [to_sibling(mine, col, 0)]

    basis_load.wait()
    for leaf in range(2):
        basis_t[leaf] = basis[pl.ds(leaf * LEAF, LEAF), :].T

    def project(q):
        for j in range(2):
            feat_loads[2 * q + j].wait()
            for leaf in range(2):
                block = jnp.dot(
                    basis_t[leaf], feat[2 * q + j, pl.ds(leaf * LEAF, LEAF), :],
                    preferred_element_type=F32,
                ).astype(BF16)
                for i in range(4):
                    coeffs[q, 4 * j + i, leaf] = block[:, i * LANES : (i + 1) * LANES]

    def send_coeffs(q):
        def one(m, carry):
            px, pz, pk = relative(m)
            ship(
                coeffs.at[q, px * 2 + pk, pz], xa.at[q, col],
                send_sem.at[0, q, m], recv_sem.at[0, q], column(px, pz, pk), row,
            )
            return carry

        lax.fori_loop(0, 16, one, 0)

    project(0)
    send_coeffs(0)
    arrived(partner, w_recv.at[0])
    w2 += [
        weights_to(win.at[partner], partner, 3, w_recv.at[2 - zl], column(right, zl, k)),
        weights_to(win.at[partner], partner, 4, w_recv.at[4 - zl], column(left, zl, k)),
    ]
    w2[2].start()
    w2[3].start()
    siblings.append(to_sibling(win.at[partner], partner, 1))
    project(1)
    send_coeffs(1)

    from_left = [column(left, z, k) for z in range(2)]
    from_right = [column(right, z, k) for z in range(2)]
    arrived(from_right[0], w_recv.at[3])
    w3 = [weights_to(win.at[from_right[0]], from_right[0], 5, w_recv.at[5], column(left, zl, k))]
    w3[0].start()
    siblings.append(to_sibling(win.at[from_right[0]], from_right[0], 2))
    arrived(from_left[1], w_recv.at[2])
    w3.append(weights_to(win.at[from_left[1]], from_left[1], 6, w_recv.at[6], column(right, zl, k)))
    w3[1].start()
    siblings.append(to_sibling(win.at[from_left[1]], from_left[1], 3))
    arrived(from_left[0], w_recv.at[1])
    siblings.append(to_sibling(win.at[from_left[0]], from_left[0], 4))
    arrived(from_right[1], w_recv.at[4])
    siblings.append(to_sibling(win.at[from_right[1]], from_right[1], 5))

    lout_load.wait()

    def gram_of(i, carry):
        rows = lout[pl.ds(i * LEAF, LEAF), :]
        product = lax.dot_general(rows, rows, (((0,), (0,)), ((), ())), preferred_element_type=F32)
        high = product.astype(BF16)
        low = (product - high.astype(F32)).astype(BF16)
        gram[i] = jnp.concatenate([high, low], axis=1)
        return carry

    lax.fori_loop(0, 16, gram_of, 0)

    far = (x + 2) % 4
    for z in range(2):
        arrived(column(far, z, k), w_recv.at[5 + z])
        siblings.append(to_sibling(win.at[column(far, z, k)], column(far, z, k), 6 + z))

    wout_load.wait()

    for level in range(LEVELS):
        for n, b in enumerate(pairs_of(level)):
            wout_t[level, n] = pair_matrix(wout[level, b], wout[level, b | 1 << level]).T

    own_load.wait()
    for copy in siblings:
        copy.wait_recv()

    def received(buffer, phase, q):
        pltpu.make_async_copy(buffer.at[q], buffer.at[q], recv_sem.at[phase, q]).wait()

    def mix(buffer, q, level, matrix):
        for n, b in enumerate(pairs_of(level)):
            p = b | 1 << level
            stack = jnp.concatenate([buffer[q, b], buffer[q, p]], axis=0)
            mixed = jnp.dot(matrix(level, n, b, p), stack, preferred_element_type=F32).astype(BF16)
            buffer[q, b] = mixed[:RANK]
            buffer[q, p] = mixed[RANK:]

    def forward_in(level, n, b, p):
        return pair_matrix(win[b, level], win[p, level])

    def forward_out(level, n, b, p):
        return pair_matrix(wout[level, b], wout[level, p])

    def backward_in(level, n, b, p):
        return win_t[level, n]

    def backward_out(level, n, b, p):
        return wout_t[level, n]

    def input_side(q, carry):
        received(xa, 0, q)
        for level in range(LEVELS):
            mix(xa, q, level, forward_in)

        def one(m, c):
            px, pz, pk = relative(m)
            to, r = spread_row(m, q)
            ship(
                xa.at[q, to], xb.at[q, row * 2 + zl],
                send_sem.at[1, q, m], recv_sem.at[1, q], to, r,
            )
            return c

        lax.fori_loop(0, 16, one, 0)
        return carry

    lax.fori_loop(0, 2, input_side, 0)

    for level in range(LEVELS):
        for n, b in enumerate(pairs_of(level)):
            win_t[level, n] = pair_matrix(win[b, level], win[b | 1 << level, level]).T

    def output_side(q, carry):
        received(xb, 1, q)
        for level in range(LEVELS):
            mix(xb, q, level, forward_out)
        for b in range(16):
            twice = jnp.concatenate([xb[q, b], xb[q, b]], axis=0)
            xb[q, b] = jnp.dot(gram[b], twice, preferred_element_type=F32).astype(BF16)
        for level in reversed(range(LEVELS)):
            mix(xb, q, level, backward_out)

        def one(m, c):
            to, r = gather_row(m, q)
            ship(
                xb.at[q, m], xr.at[q, col],
                send_sem.at[2, q, m], recv_sem.at[2, q], to, r,
            )
            return c

        lax.fori_loop(0, 16, one, 0)
        return carry

    lax.fori_loop(0, 2, output_side, 0)

    def input_side_back(q, carry):
        received(xr, 2, q)
        for level in reversed(range(LEVELS)):
            mix(xr, q, level, backward_in)

        def one(m, c):
            px, pz, pk = relative(m)
            to = column(px, pz, pk)
            ship(
                xr.at[q, to], home.at[q, x * 2 + k, zl],
                send_sem.at[3, q, m], recv_sem.at[3, q], to, row,
            )
            return c

        lax.fori_loop(0, 16, one, 0)
        return carry

    lax.fori_loop(0, 2, input_side_back, 0)

    for q in range(2):
        received(home, 3, q)
        outs = [
            pltpu.make_async_copy(
                home.at[q, j, leaf],
                returned.at[leaf, :, pl.ds((q * 8 + j) * LANES, LANES)],
                out_sem.at[q, j, leaf],
            )
            for j in range(8)
            for leaf in range(2)
        ]
        for copy in outs:
            copy.start()
        for copy in outs:
            copy.wait()

    w1.wait_send()
    for copy in w2 + w3 + siblings:
        copy.wait_send()

    def drain(src, send, c, r):
        here = jnp.logical_and(c == col, r == row)

        @pl.when(jnp.logical_not(here))
        def _():
            pltpu.make_async_remote_copy(
                src_ref=src, dst_ref=src, send_sem=send, recv_sem=send,
                device_id={"col": c, "row": r}, device_id_type=MESH,
            ).wait_send()

    def finish(m, carry):
        for q in range(2):
            px, pz, pk = relative(m)
            to = column(px, pz, pk)
            drain(coeffs.at[q, px * 2 + pk, pz], send_sem.at[0, q, m], to, row)
            c, r = spread_row(m, q)
            drain(xa.at[q, c], send_sem.at[1, q, m], c, r)
            c, r = gather_row(m, q)
            drain(xb.at[q, m], send_sem.at[2, q, m], c, r)
            drain(xr.at[q, to], send_sem.at[3, q, m], to, row)
        return carry

    lax.fori_loop(0, 16, finish, 0)


def operator(features, leaf_in, mix_in, mix_out, leaf_out):
    hbm = pl.BlockSpec(memory_space=pltpu.HBM)
    dma = pltpu.SemaphoreType.DMA
    return pl.pallas_call(
        operator_kernel,
        out_shape=jax.ShapeDtypeStruct((2, RANK, features.shape[1]), BF16),
        in_specs=[hbm] * 5,
        out_specs=hbm,
        scratch_shapes=[
            pltpu.VMEM((4, 2 * LEAF, 512), BF16),
            pltpu.VMEM((2 * LEAF, RANK), BF16),
            pltpu.VMEM((2, RANK, LEAF), BF16),
            pltpu.VMEM((16, LEVELS, RANK, 2 * RANK), BF16),
            pltpu.VMEM((LEVELS, 8, 2 * RANK, 2 * RANK), BF16),
            pltpu.VMEM((LEVELS, 16, RANK, 2 * RANK), BF16),
            pltpu.VMEM((LEVELS, 8, 2 * RANK, 2 * RANK), BF16),
            pltpu.VMEM((16 * LEAF, RANK), BF16),
            pltpu.VMEM((16, RANK, 2 * RANK), BF16),
            pltpu.VMEM((2, 8, 2, RANK, LANES), BF16),
            pltpu.VMEM((2, 16, RANK, LANES), BF16),
            pltpu.VMEM((2, 16, RANK, LANES), BF16),
            pltpu.VMEM((2, 16, RANK, LANES), BF16),
            pltpu.VMEM((2, 8, 2, RANK, LANES), BF16),
            dma((8,)), dma((8,)), dma((8,)), dma((1,)), dma((8,)), dma((8,)),
            dma((4, 2, 16)), dma((4, 2)), dma((2, 8, 2)),
        ],
        compiler_params=pltpu.CompilerParams(
            collective_id=0, has_side_effects=True, vmem_limit_bytes=56 << 20
        ),
        name="operator",
    )(features, leaf_in, mix_in, mix_out, leaf_out)


def body(features, leaf_in, mix_in, mix_out, leaf_out):
    returned = operator(features, leaf_in, mix_in, mix_out, leaf_out)
    leaf_rows = leaf_in.reshape(2, LEAF, RANK)
    result = jnp.einsum("bmk,bkr->bmr", leaf_rows, returned, preferred_element_type=F32)
    return result.astype(BF16).reshape(features.shape)


def solution(mesh):
    in_specs = (
        P(("col", "row"), None),
        P(("col", "row"), None),
        P(None, ("col", "row"), None, None),
        P(None, "col", None, None),
        P("col", None),
    )
    out_specs = P(("col", "row"), None)
    return jax.shard_map(body, mesh=mesh, in_specs=in_specs, out_specs=out_specs, check_vma=False)
```

```python
import jax
import jax.numpy as jnp
from jax import lax
from jax.experimental import pallas as pl
from jax.experimental.pallas import tpu as pltpu
from jax.sharding import PartitionSpec as P

LEAF = 1024
RANK = 128
LANES = 128
MESH = pl.DeviceIdType.MESH
F32 = jnp.float32
BF16 = jnp.bfloat16
LEVELS = 4


def pairs_of(bit):
    return [b for b in range(16) if not b >> bit & 1]


def pair_matrix(top, bottom):
    swapped = jnp.concatenate([bottom[:, RANK:], bottom[:, :RANK]], axis=1)
    return jnp.concatenate([top, swapped], axis=0)


def column(x, zl, k):
    return x * 4 + zl * 2 + k


def operator_kernel(
    features, leaf_in, mix_in, mix_out, leaf_out, returned,
    feat, basis, basis_t, win, near_t, far_t, wout, wout_t, lout, gram,
    coeffs, xz, xa, xb, xr, zr,
    load_sem, w_send, w_recv, sib_send, sib_recv, send_sem, recv_sem,
):
    col, row = lax.axis_index("col"), lax.axis_index("row")
    x, zl, k = col // 4, col // 2 % 2, col % 2
    zh, y = row // 4, row % 4
    x_hi, x_lo, y_hi, y_lo = x // 2, x % 2, y // 2, y % 2
    right, left = (x + 1) % 4, (x + 3) % 4

    feat_loads = [
        pltpu.make_async_copy(
            features.at[:, pl.ds(j * 512, 512)], feat.at[j], load_sem.at[j]
        )
        for j in range(4)
    ]
    basis_load = pltpu.make_async_copy(leaf_in, basis, load_sem.at[4])
    wout_load = pltpu.make_async_copy(mix_out, wout, load_sem.at[5])
    lout_load = pltpu.make_async_copy(leaf_out, lout, load_sem.at[6])
    own_load = pltpu.make_async_copy(mix_in.at[:, zl], win.at[col], load_sem.at[7])
    def relative(m):
        px = (x + m + 1) % 4
        pz = (zl + m + m // 4) % 2
        pk = (k + m // 2 + m // 8) % 2
        return px, pz, pk

    def spread_row(m):
        px, pz, pk = relative(m)
        py = (x_lo + px) % 2 * 2 + (x_hi + pk) % 2
        return column(px, pz, pk), k * 4 + py

    def gather_row(m):
        px = (y_lo + k) % 2 * 2 + (y_hi + x) % 2
        return column(px, m % 2, zh), m // 2

    barrier = pltpu.get_barrier_semaphore()

    def greet(m, carry):
        for c, r in (spread_row(m), gather_row(m)):
            pl.semaphore_signal(barrier, device_id={"col": c, "row": r}, device_id_type=MESH)
        return carry

    def near(m):
        pz, pk = (zl + m + 1) % 2, (k + m // 2 + 1) % 2
        return pz, pk, column(x, pz, pk)

    def across(m):
        px = (x + m + 1) % 4
        return px, column(px, zl, k)

    def greet_group(m, carry):
        for c in (near(m)[-1], across(m)[-1]):
            pl.semaphore_signal(barrier, device_id={"col": c, "row": row}, device_id_type=MESH)
        return carry

    for load in [basis_load, *feat_loads[:2]]:
        load.start()
    lax.fori_loop(0, 4, greet_group, 0)
    lax.fori_loop(0, 16, greet, 0)
    pl.semaphore_wait(barrier, 40)

    def ship(src, dst, send, recv, c, r):
        here = jnp.logical_and(c == col, r == row)

        @pl.when(here)
        def _():
            pltpu.make_async_copy(src, dst, recv).start()

        @pl.when(jnp.logical_not(here))
        def _():
            pltpu.make_async_remote_copy(
                src_ref=src, dst_ref=dst, send_sem=send, recv_sem=recv,
                device_id={"col": c, "row": r}, device_id_type=MESH,
            ).start()

    early, late = pl.ds(0, 2), pl.ds(2, 2)

    def weights_to(src, slot, levels, n, recv, c):
        copy = pltpu.make_async_remote_copy(
            src_ref=src, dst_ref=win.at[slot, levels], send_sem=w_send.at[n], recv_sem=recv,
            device_id={"col": c}, device_id_type=MESH,
        )
        copy.start()
        return copy

    def arrived(slot, levels, sem):
        block = win.at[slot, levels]
        pltpu.make_async_copy(block, block, sem).wait()

    siblings = []

    def to_sibling(src, slot, levels):
        n = len(siblings)
        copy = pltpu.make_async_remote_copy(
            src_ref=src, dst_ref=win.at[slot, levels],
            send_sem=sib_send.at[n], recv_sem=sib_recv.at[n],
            device_id={"col": column(x, zl, 1 - k)}, device_id_type=MESH,
        )
        copy.start()
        siblings.append(copy)

    partner = column(x, 1 - zl, k)
    gives = [
        weights_to(mix_in.at[late, 1 - zl], col, late, 0, w_recv.at[0], partner),
        weights_to(mix_in.at[late, zl], col, late, 1, w_recv.at[1 + zl], column(right, zl, k)),
        weights_to(mix_in.at[late, zl], col, late, 2, w_recv.at[3 + zl], column(left, zl, k)),
        weights_to(mix_in.at[early, 1 - zl], col, early, 7, w_recv.at[7], partner),
    ]
    to_sibling(mix_in.at[early, zl], col, early)
    for load in [*feat_loads[2:], own_load]:
        load.start()

    basis_load.wait()
    for leaf in range(2):
        basis_t[leaf] = basis[pl.ds(leaf * LEAF, LEAF), :].T

    def project(q):
        for j in range(2):
            feat_loads[2 * q + j].wait()
            for leaf in range(2):
                block = jnp.dot(
                    basis_t[leaf], feat[2 * q + j, pl.ds(leaf * LEAF, LEAF), :],
                    preferred_element_type=F32,
                ).astype(BF16)
                for i in range(4):
                    coeffs[q, i % 2, leaf, 2 * j + i // 2] = block[:, i * LANES : (i + 1) * LANES]

    def send_coeffs(q):
        def one(m, carry):
            pz, pk, to = near(m)
            ship(
                coeffs.at[q, pk, pz], xz.at[q, zl * 2 + k],
                send_sem.at[0, q, m], recv_sem.at[0, q], to, row,
            )
            return carry

        lax.fori_loop(0, 4, one, 0)

    project(0)
    send_coeffs(0)
    arrived(partner, late, w_recv.at[0])
    block = win.at[partner, late]
    gives += [
        weights_to(block, partner, late, 3, w_recv.at[2 - zl], column(right, zl, k)),
        weights_to(block, partner, late, 4, w_recv.at[4 - zl], column(left, zl, k)),
    ]
    arrived(partner, early, w_recv.at[7])
    to_sibling(win.at[partner, early], partner, early)
    project(1)
    send_coeffs(1)
    lout_load.start()
    wout_load.start()
    to_sibling(mix_in.at[late, zl], col, late)
    to_sibling(win.at[partner, late], partner, late)

    from_left = [column(left, z, k) for z in range(2)]
    from_right = [column(right, z, k) for z in range(2)]
    for slot, sem, n, c in (
        (from_right[0], 3, 5, column(left, zl, k)),
        (from_left[1], 2, 6, column(right, zl, k)),
    ):
        arrived(slot, late, w_recv.at[sem])
        gives.append(weights_to(win.at[slot, late], slot, late, n, w_recv.at[n], c))
        to_sibling(win.at[slot, late], slot, late)
    for slot, sem in ((from_left[0], 1), (from_right[1], 4)):
        arrived(slot, late, w_recv.at[sem])
        to_sibling(win.at[slot, late], slot, late)

    def received(buffer, phase, q):
        pltpu.make_async_copy(buffer.at[q], buffer.at[q], recv_sem.at[phase, q]).wait()

    def mix_near(buffer, q, level, matrix):
        for n, b in enumerate(b for b in range(4) if not b >> level & 1):
            p = b | 1 << level
            for i in (0, 2):
                stack = jnp.concatenate(
                    [
                        jnp.concatenate([buffer[q, c, i], buffer[q, c, i + 1]], axis=1)
                        for c in (b, p)
                    ],
                    axis=0,
                )
                mixed = jnp.dot(
                    matrix(level, n, b, p), stack, preferred_element_type=F32
                ).astype(BF16)
                for c, part in ((b, mixed[:RANK]), (p, mixed[RANK:])):
                    buffer[q, c, i] = part[:, :LANES]
                    buffer[q, c, i + 1] = part[:, LANES:]

    def near_matrix(level, n, b, p):
        return pair_matrix(win[x * 4 + b, level], win[x * 4 + p, level])

    own_load.wait()
    for copy in siblings[:2]:
        copy.wait_recv()

    def near_side(q, carry):
        received(xz, 0, q)
        for level in range(2):
            mix_near(xz, q, level, near_matrix)

        def one(m, c):
            px, to = across(m)
            ship(
                xz.at[q, :, px], xa.at[q, pl.ds(x * 4, 4)],
                send_sem.at[1, q, m], recv_sem.at[1, q], to, row,
            )
            return c

        lax.fori_loop(0, 4, one, 0)
        return carry

    lax.fori_loop(0, 2, near_side, 0)

    far = (x + 2) % 4
    for z in range(2):
        slot = column(far, z, k)
        arrived(slot, late, w_recv.at[5 + z])
        to_sibling(win.at[slot, late], slot, late)

    lout_load.wait()

    def gram_of(i, carry):
        rows = lout[pl.ds(i * LEAF, LEAF), :]
        product = lax.dot_general(rows, rows, (((0,), (0,)), ((), ())), preferred_element_type=F32)
        high = product.astype(BF16)
        low = (product - high.astype(F32)).astype(BF16)
        gram[i] = jnp.concatenate([high, low], axis=1)
        return carry

    lax.fori_loop(0, 16, gram_of, 0)

    wout_load.wait()

    for level in range(LEVELS):
        for n, b in enumerate(pairs_of(level)):
            wout_t[level, n] = pair_matrix(wout[level, b], wout[level, b | 1 << level]).T

    for copy in siblings[2:]:
        copy.wait_recv()

    def mix(buffer, q, level, matrix):
        for n, b in enumerate(pairs_of(level)):
            p = b | 1 << level
            stack = jnp.concatenate([buffer[q, b], buffer[q, p]], axis=0)
            mixed = jnp.dot(matrix(level, n, b, p), stack, preferred_element_type=F32).astype(BF16)
            buffer[q, b] = mixed[:RANK]
            buffer[q, p] = mixed[RANK:]

    def forward_in(level, n, b, p):
        return pair_matrix(win[b, level], win[p, level])

    def forward_out(level, n, b, p):
        return pair_matrix(wout[level, b], wout[level, p])

    def backward_in(level, n, b, p):
        return far_t[level - 2, n]

    def backward_near(level, n, b, p):
        return near_t[level, n]

    def backward_out(level, n, b, p):
        return wout_t[level, n]

    def input_side(q, carry):
        received(xa, 1, q)
        for level in (2, 3):
            mix(xa, q, level, forward_in)

        def one(m, c):
            px, pz, pk = relative(m)
            to, r = spread_row(m)
            ship(
                xa.at[q, to], xb.at[q, row * 2 + zl],
                send_sem.at[2, q, m], recv_sem.at[2, q], to, r,
            )
            return c

        lax.fori_loop(0, 16, one, 0)
        return carry

    lax.fori_loop(0, 2, input_side, 0)

    for level in (2, 3):
        for n, b in enumerate(pairs_of(level)):
            far_t[level - 2, n] = pair_matrix(win[b, level], win[b | 1 << level, level]).T
    for level in range(2):
        for n, b in enumerate(b for b in range(4) if not b >> level & 1):
            near_t[level, n] = near_matrix(level, n, b, b | 1 << level).T

    def output_side(q, carry):
        received(xb, 2, q)
        for level in range(LEVELS):
            mix(xb, q, level, forward_out)
        for b in range(16):
            twice = jnp.concatenate([xb[q, b], xb[q, b]], axis=0)
            xb[q, b] = jnp.dot(gram[b], twice, preferred_element_type=F32).astype(BF16)
        for level in reversed(range(LEVELS)):
            mix(xb, q, level, backward_out)

        def one(m, c):
            to, r = gather_row(m)
            ship(
                xb.at[q, m], xr.at[q, col],
                send_sem.at[3, q, m], recv_sem.at[3, q], to, r,
            )
            return c

        lax.fori_loop(0, 16, one, 0)
        return carry

    lax.fori_loop(0, 2, output_side, 0)

    def input_side_back(q, carry):
        received(xr, 3, q)
        for level in (3, 2):
            mix(xr, q, level, backward_in)

        def one(m, c):
            px, to = across(m)
            ship(
                xr.at[q, pl.ds(px * 4, 4)], zr.at[q, :, x],
                send_sem.at[4, q, m], recv_sem.at[4, q], to, row,
            )
            return c

        lax.fori_loop(0, 4, one, 0)
        return carry

    lax.fori_loop(0, 2, input_side_back, 0)

    def near_side_back(q, carry):
        received(zr, 4, q)
        for level in (1, 0):
            mix_near(zr, q, level, backward_near)

        def one(m, c):
            pz, pk, to = near(m)
            ship(
                zr.at[q, pz * 2 + pk], returned.at[q, k, zl],
                send_sem.at[5, q, m], recv_sem.at[5, q], to, row,
            )
            return c

        lax.fori_loop(0, 4, one, 0)
        return carry

    lax.fori_loop(0, 2, near_side_back, 0)

    for q in range(2):
        received(returned, 5, q)

    for copy in gives + siblings:
        copy.wait_send()

    def drain(src, send, c, r):
        here = jnp.logical_and(c == col, r == row)

        @pl.when(jnp.logical_not(here))
        def _():
            pltpu.make_async_remote_copy(
                src_ref=src, dst_ref=src, send_sem=send, recv_sem=send,
                device_id={"col": c, "row": r}, device_id_type=MESH,
            ).wait_send()

    def finish(m, carry):
        for q in range(2):
            c, r = spread_row(m)
            drain(xa.at[q, c], send_sem.at[2, q, m], c, r)
            c, r = gather_row(m)
            drain(xb.at[q, m], send_sem.at[3, q, m], c, r)
        return carry

    lax.fori_loop(0, 16, finish, 0)

    def finish_group(m, carry):
        for q in range(2):
            pz, pk, to = near(m)
            drain(coeffs.at[q, pk, pz], send_sem.at[0, q, m], to, row)
            drain(zr.at[q, pz * 2 + pk], send_sem.at[5, q, m], to, row)
            px, to = across(m)
            drain(xz.at[q, :, px], send_sem.at[1, q, m], to, row)
            drain(xr.at[q, pl.ds(px * 4, 4)], send_sem.at[4, q, m], to, row)
        return carry

    lax.fori_loop(0, 4, finish_group, 0)


def operator(features, leaf_in, mix_in, mix_out, leaf_out):
    hbm = pl.BlockSpec(memory_space=pltpu.HBM)
    dma = pltpu.SemaphoreType.DMA
    return pl.pallas_call(
        operator_kernel,
        out_shape=jax.ShapeDtypeStruct((2, 2, 2, 4, RANK, LANES), BF16),
        in_specs=[hbm] * 5,
        out_specs=hbm,
        scratch_shapes=[
            pltpu.VMEM((4, 2 * LEAF, 512), BF16),
            pltpu.VMEM((2 * LEAF, RANK), BF16),
            pltpu.VMEM((2, RANK, LEAF), BF16),
            pltpu.VMEM((16, LEVELS, RANK, 2 * RANK), BF16),
            pltpu.VMEM((2, 2, 2 * RANK, 2 * RANK), BF16),
            pltpu.VMEM((2, 8, 2 * RANK, 2 * RANK), BF16),
            pltpu.VMEM((LEVELS, 16, RANK, 2 * RANK), BF16),
            pltpu.VMEM((LEVELS, 8, 2 * RANK, 2 * RANK), BF16),
            pltpu.VMEM((16 * LEAF, RANK), BF16),
            pltpu.VMEM((16, RANK, 2 * RANK), BF16),
            pltpu.VMEM((2, 2, 2, 4, RANK, LANES), BF16),
            pltpu.VMEM((2, 4, 4, RANK, LANES), BF16),
            pltpu.VMEM((2, 16, RANK, LANES), BF16),
            pltpu.VMEM((2, 16, RANK, LANES), BF16),
            pltpu.VMEM((2, 16, RANK, LANES), BF16),
            pltpu.VMEM((2, 4, 4, RANK, LANES), BF16),
            dma((8,)), dma((8,)), dma((8,)), dma((10,)), dma((10,)),
            dma((6, 2, 16)), dma((6, 2)),
        ],
        compiler_params=pltpu.CompilerParams(
            collective_id=0, has_side_effects=True, vmem_limit_bytes=56 << 20
        ),
        name="operator",
    )(features, leaf_in, mix_in, mix_out, leaf_out)


def expand_kernel(rows_in, blocks_in, out, rows, blocks, wide, sems):
    loads = [
        pltpu.make_async_copy(rows_in, rows, sems.at[0]),
        pltpu.make_async_copy(blocks_in, blocks, sems.at[1]),
    ]
    for load in loads:
        load.start()
    for load in loads:
        load.wait()
    stores = []
    for leaf in range(2):
        here = pl.ds(leaf * LEAF, LEAF)
        for part in range(4):
            for i in range(2):
                q, side = part // 2, part % 2 * 2 + i
                columns = jnp.concatenate(
                    [blocks[q, 0, leaf, side], blocks[q, 1, leaf, side]], axis=1
                )
                wide[here, pl.ds(part * 512 + i * 256, 256)] = jnp.dot(
                    rows[here, :], columns, preferred_element_type=F32
                ).astype(BF16)
            tile = pl.ds(part * 512, 512)
            store = pltpu.make_async_copy(
                wide.at[here, tile], out.at[here, tile], sems.at[2 + len(stores)]
            )
            store.start()
            stores.append(store)
    for store in stores:
        store.wait()


def expand(leaf_in, returned, columns):
    hbm = pl.BlockSpec(memory_space=pltpu.HBM)
    return pl.pallas_call(
        expand_kernel,
        out_shape=jax.ShapeDtypeStruct((2 * LEAF, columns), BF16),
        in_specs=[hbm, hbm],
        out_specs=hbm,
        scratch_shapes=[
            pltpu.VMEM((2 * LEAF, RANK), BF16),
            pltpu.VMEM(returned.shape, BF16),
            pltpu.VMEM((2 * LEAF, columns), BF16),
            pltpu.SemaphoreType.DMA((10,)),
        ],
        compiler_params=pltpu.CompilerParams(vmem_limit_bytes=58 << 20),
        name="expand",
    )(leaf_in, returned)


def body(features, leaf_in, mix_in, mix_out, leaf_out):
    returned = operator(features, leaf_in, mix_in, mix_out, leaf_out)
    return expand(leaf_in, returned, features.shape[1])


def solution(mesh):
    in_specs = (
        P(("col", "row"), None),
        P(("col", "row"), None),
        P(None, ("col", "row"), None, None),
        P(None, "col", None, None),
        P("col", None),
    )
    out_specs = P(("col", "row"), None)
    return jax.shard_map(body, mesh=mesh, in_specs=in_specs, out_specs=out_specs, check_vma=False)
```

```python
import jax
import jax.numpy as jnp
from jax import lax
from jax.experimental import pallas as pl
from jax.experimental.pallas import tpu as pltpu
from jax.sharding import PartitionSpec as P

LEAF = 1024
RANK = 128
LANES = 128
MESH = pl.DeviceIdType.MESH
F32 = jnp.float32
BF16 = jnp.bfloat16
LEVELS = 4


def pairs_of(bit):
    return [b for b in range(16) if not b >> bit & 1]


def pair_matrix(top, bottom):
    swapped = jnp.concatenate([bottom[:, RANK:], bottom[:, :RANK]], axis=1)
    return jnp.concatenate([top, swapped], axis=0)


def column(x, zl, k):
    return x * 4 + zl * 2 + k


def operator_kernel(
    features, leaf_in, mix_in, mix_out, leaf_out, returned,
    feat, basis, basis_t, win, near_t, far_t, wout, wout_t, lout, gram,
    coeffs, xz, xa, xb, xr, zr,
    load_sem, w_send, w_recv, sib_send, sib_recv, send_sem, recv_sem,
):
    col, row = lax.axis_index("col"), lax.axis_index("row")
    x, zl, k = col // 4, col // 2 % 2, col % 2
    zh, y = row // 4, row % 4
    x_hi, x_lo, y_hi, y_lo = x // 2, x % 2, y // 2, y % 2
    right, left = (x + 1) % 4, (x + 3) % 4

    feat_loads = [
        pltpu.make_async_copy(
            features.at[:, pl.ds(j * 512, 512)], feat.at[j], load_sem.at[j]
        )
        for j in range(4)
    ]
    basis_load = pltpu.make_async_copy(leaf_in, basis, load_sem.at[4])
    wout_load = pltpu.make_async_copy(mix_out, wout, load_sem.at[5])
    lout_load = pltpu.make_async_copy(leaf_out, lout, load_sem.at[6])
    own_load = pltpu.make_async_copy(mix_in.at[:, zl], win.at[col], load_sem.at[7])
    def relative(m):
        px = (x + m + 1) % 4
        pz = (zl + m + m // 4) % 2
        pk = (k + m // 2 + m // 8) % 2
        return px, pz, pk

    def spread_row(m):
        px, pz, pk = relative(m)
        py = (x_lo + px) % 2 * 2 + (x_hi + pk) % 2
        return column(px, pz, pk), k * 4 + py

    def gather_row(m):
        px = (y_lo + k) % 2 * 2 + (y_hi + x) % 2
        pz, py, ph = m % 2, m // 2 % 4, m // 8
        return column(px, pz, zh), ph * 4 + py, (ph * 4 + py) * 2 + pz

    barrier = pltpu.get_barrier_semaphore()

    def greet(m, carry):
        for c, r in (spread_row(m), gather_row(m)[:2]):
            pl.semaphore_signal(barrier, device_id={"col": c, "row": r}, device_id_type=MESH)
        return carry

    def near(m):
        pz, pk = (zl + m + 1) % 2, (k + m // 2 + 1) % 2
        return pz, pk, column(x, pz, pk)

    def across(m):
        px = (x + m + 1) % 4
        return px, column(px, zl, k)

    def greet_group(m, carry):
        for c in (near(m)[-1], across(m)[-1]):
            pl.semaphore_signal(barrier, device_id={"col": c, "row": row}, device_id_type=MESH)
        return carry

    for load in [basis_load, *feat_loads[:2]]:
        load.start()
    lax.fori_loop(0, 4, greet_group, 0)
    lax.fori_loop(0, 16, greet, 0)
    pl.semaphore_wait(barrier, 40)

    def ship(src, dst, send, recv, c, r):
        here = jnp.logical_and(c == col, r == row)

        @pl.when(here)
        def _():
            pltpu.make_async_copy(src, dst, recv).start()

        @pl.when(jnp.logical_not(here))
        def _():
            pltpu.make_async_remote_copy(
                src_ref=src, dst_ref=dst, send_sem=send, recv_sem=recv,
                device_id={"col": c, "row": r}, device_id_type=MESH,
            ).start()

    early, late = pl.ds(0, 2), pl.ds(2, 2)

    def weights_to(src, slot, levels, n, recv, c):
        copy = pltpu.make_async_remote_copy(
            src_ref=src, dst_ref=win.at[slot, levels], send_sem=w_send.at[n], recv_sem=recv,
            device_id={"col": c}, device_id_type=MESH,
        )
        copy.start()
        return copy

    def arrived(slot, levels, sem):
        block = win.at[slot, levels]
        pltpu.make_async_copy(block, block, sem).wait()

    siblings = []

    def to_sibling(src, slot, levels):
        n = len(siblings)
        copy = pltpu.make_async_remote_copy(
            src_ref=src, dst_ref=win.at[slot, levels],
            send_sem=sib_send.at[n], recv_sem=sib_recv.at[n],
            device_id={"col": column(x, zl, 1 - k)}, device_id_type=MESH,
        )
        copy.start()
        siblings.append(copy)

    partner = column(x, 1 - zl, k)
    gives = [
        weights_to(mix_in.at[late, 1 - zl], col, late, 0, w_recv.at[0], partner),
        weights_to(mix_in.at[late, zl], col, late, 1, w_recv.at[1 + zl], column(right, zl, k)),
        weights_to(mix_in.at[late, zl], col, late, 2, w_recv.at[3 + zl], column(left, zl, k)),
        weights_to(mix_in.at[early, 1 - zl], col, early, 7, w_recv.at[7], partner),
    ]
    to_sibling(mix_in.at[early, zl], col, early)
    for load in [*feat_loads[2:], own_load]:
        load.start()

    basis_load.wait()
    for leaf in range(2):
        basis_t[leaf] = basis[pl.ds(leaf * LEAF, LEAF), :].T

    def project(q):
        for j in range(2):
            feat_loads[2 * q + j].wait()
            for leaf in range(2):
                block = jnp.dot(
                    basis_t[leaf], feat[2 * q + j, pl.ds(leaf * LEAF, LEAF), :],
                    preferred_element_type=F32,
                ).astype(BF16)
                for i in range(4):
                    coeffs[q, i % 2, leaf, 2 * j + i // 2] = block[:, i * LANES : (i + 1) * LANES]

    def send_coeffs(q):
        def one(m, carry):
            pz, pk, to = near(m)
            ship(
                coeffs.at[q, pk, pz], xz.at[q, zl * 2 + k],
                send_sem.at[0, q, m], recv_sem.at[0, q], to, row,
            )
            return carry

        lax.fori_loop(0, 4, one, 0)

    project(0)
    send_coeffs(0)
    arrived(partner, late, w_recv.at[0])
    block = win.at[partner, late]
    gives += [
        weights_to(block, partner, late, 3, w_recv.at[2 - zl], column(right, zl, k)),
        weights_to(block, partner, late, 4, w_recv.at[4 - zl], column(left, zl, k)),
    ]
    project(1)
    send_coeffs(1)
    lout_load.start()
    wout_load.start()
    arrived(partner, early, w_recv.at[7])
    to_sibling(win.at[partner, early], partner, early)
    to_sibling(mix_in.at[late, zl], col, late)
    to_sibling(win.at[partner, late], partner, late)

    from_left = [column(left, z, k) for z in range(2)]
    from_right = [column(right, z, k) for z in range(2)]
    for slot, sem, n, c in (
        (from_right[0], 3, 5, column(left, zl, k)),
        (from_left[1], 2, 6, column(right, zl, k)),
    ):
        arrived(slot, late, w_recv.at[sem])
        gives.append(weights_to(win.at[slot, late], slot, late, n, w_recv.at[n], c))
        to_sibling(win.at[slot, late], slot, late)
    for slot, sem in ((from_left[0], 1), (from_right[1], 4)):
        arrived(slot, late, w_recv.at[sem])
        to_sibling(win.at[slot, late], slot, late)

    def received(buffer, phase, q):
        pltpu.make_async_copy(buffer.at[q], buffer.at[q], recv_sem.at[phase, q]).wait()

    def mix_near(buffer, q, level, matrix):
        for n, b in enumerate(b for b in range(4) if not b >> level & 1):
            p = b | 1 << level
            for i in (0, 2):
                stack = jnp.concatenate(
                    [
                        jnp.concatenate([buffer[q, c, i], buffer[q, c, i + 1]], axis=1)
                        for c in (b, p)
                    ],
                    axis=0,
                )
                mixed = jnp.dot(
                    matrix(level, n, b, p), stack, preferred_element_type=F32
                ).astype(BF16)
                for c, part in ((b, mixed[:RANK]), (p, mixed[RANK:])):
                    buffer[q, c, i] = part[:, :LANES]
                    buffer[q, c, i + 1] = part[:, LANES:]

    def near_matrix(level, n, b, p):
        return pair_matrix(win[x * 4 + b, level], win[x * 4 + p, level])

    own_load.wait()
    for copy in siblings[:2]:
        copy.wait_recv()

    def near_side(q, carry):
        received(xz, 0, q)
        for level in range(2):
            mix_near(xz, q, level, near_matrix)

        def one(m, c):
            px, to = across(m)
            ship(
                xz.at[q, :, px], xa.at[q, pl.ds(x * 4, 4)],
                send_sem.at[1, q, m], recv_sem.at[1, q], to, row,
            )
            return c

        lax.fori_loop(0, 4, one, 0)
        return carry

    near_side(0, 0)

    far = (x + 2) % 4
    for z in range(2):
        slot = column(far, z, k)
        arrived(slot, late, w_recv.at[5 + z])
        to_sibling(win.at[slot, late], slot, late)

    lout_load.wait()

    def gram_of(i, carry):
        rows = lout[pl.ds(i * LEAF, LEAF), :]
        product = lax.dot_general(rows, rows, (((0,), (0,)), ((), ())), preferred_element_type=F32)
        high = product.astype(BF16)
        low = (product - high.astype(F32)).astype(BF16)
        gram[i] = jnp.concatenate([high, low], axis=1)
        return carry

    lax.fori_loop(0, 16, gram_of, 0)
    near_side(1, 0)

    wout_load.wait()

    for level in range(LEVELS):
        for n, b in enumerate(pairs_of(level)):
            wout_t[level, n] = pair_matrix(wout[level, b], wout[level, b | 1 << level]).T

    for copy in siblings[2:]:
        copy.wait_recv()

    def mix(buffer, q, level, matrix):
        for n, b in enumerate(pairs_of(level)):
            p = b | 1 << level
            stack = jnp.concatenate([buffer[q, b], buffer[q, p]], axis=0)
            mixed = jnp.dot(matrix(level, n, b, p), stack, preferred_element_type=F32).astype(BF16)
            buffer[q, b] = mixed[:RANK]
            buffer[q, p] = mixed[RANK:]

    def forward_in(level, n, b, p):
        return pair_matrix(win[b, level], win[p, level])

    def forward_out(level, n, b, p):
        return pair_matrix(wout[level, b], wout[level, p])

    def backward_in(level, n, b, p):
        return far_t[level - 2, n]

    def backward_near(level, n, b, p):
        return near_t[level, n]

    def backward_out(level, n, b, p):
        return wout_t[level, n]

    def input_side(q, carry):
        received(xa, 1, q)
        for level in (2, 3):
            mix(xa, q, level, forward_in)

        def one(m, c):
            px, pz, pk = relative(m)
            to, r = spread_row(m)
            ship(
                xa.at[q, to], xb.at[q, row * 2 + zl],
                send_sem.at[2, q, m], recv_sem.at[2, q], to, r,
            )
            return c

        lax.fori_loop(0, 16, one, 0)
        return carry

    lax.fori_loop(0, 2, input_side, 0)

    for level in (2, 3):
        for n, b in enumerate(pairs_of(level)):
            far_t[level - 2, n] = pair_matrix(win[b, level], win[b | 1 << level, level]).T
    for level in range(2):
        for n, b in enumerate(b for b in range(4) if not b >> level & 1):
            near_t[level, n] = near_matrix(level, n, b, b | 1 << level).T

    def output_side(q, carry):
        received(xb, 2, q)
        for level in range(LEVELS):
            mix(xb, q, level, forward_out)
        for b in range(16):
            twice = jnp.concatenate([xb[q, b], xb[q, b]], axis=0)
            xb[q, b] = jnp.dot(gram[b], twice, preferred_element_type=F32).astype(BF16)
        for level in reversed(range(LEVELS)):
            mix(xb, q, level, backward_out)

        def one(m, c):
            to, r, b = gather_row(m)
            ship(
                xb.at[q, b], xr.at[q, col],
                send_sem.at[3, q, m], recv_sem.at[3, q], to, r,
            )
            return c

        lax.fori_loop(0, 16, one, 0)
        return carry

    lax.fori_loop(0, 2, output_side, 0)

    def input_side_back(q, carry):
        received(xr, 3, q)
        for level in (3, 2):
            mix(xr, q, level, backward_in)

        def one(m, c):
            px, to = across(m)
            ship(
                xr.at[q, pl.ds(px * 4, 4)], zr.at[q, :, x],
                send_sem.at[4, q, m], recv_sem.at[4, q], to, row,
            )
            return c

        lax.fori_loop(0, 4, one, 0)
        return carry

    lax.fori_loop(0, 2, input_side_back, 0)

    def near_side_back(q, carry):
        received(zr, 4, q)
        for level in (1, 0):
            mix_near(zr, q, level, backward_near)

        def one(m, c):
            pz, pk, to = near(m)
            ship(
                zr.at[q, pz * 2 + pk], returned.at[q, k, zl],
                send_sem.at[5, q, m], recv_sem.at[5, q], to, row,
            )
            return c

        lax.fori_loop(0, 4, one, 0)
        return carry

    lax.fori_loop(0, 2, near_side_back, 0)

    for q in range(2):
        received(returned, 5, q)

    for copy in gives + siblings:
        copy.wait_send()

    def drain(src, send, c, r):
        here = jnp.logical_and(c == col, r == row)

        @pl.when(jnp.logical_not(here))
        def _():
            pltpu.make_async_remote_copy(
                src_ref=src, dst_ref=src, send_sem=send, recv_sem=send,
                device_id={"col": c, "row": r}, device_id_type=MESH,
            ).wait_send()

    def finish(m, carry):
        for q in range(2):
            c, r = spread_row(m)
            drain(xa.at[q, c], send_sem.at[2, q, m], c, r)
            c, r, b = gather_row(m)
            drain(xb.at[q, b], send_sem.at[3, q, m], c, r)
        return carry

    lax.fori_loop(0, 16, finish, 0)

    def finish_group(m, carry):
        for q in range(2):
            pz, pk, to = near(m)
            drain(coeffs.at[q, pk, pz], send_sem.at[0, q, m], to, row)
            drain(zr.at[q, pz * 2 + pk], send_sem.at[5, q, m], to, row)
            px, to = across(m)
            drain(xz.at[q, :, px], send_sem.at[1, q, m], to, row)
            drain(xr.at[q, pl.ds(px * 4, 4)], send_sem.at[4, q, m], to, row)
        return carry

    lax.fori_loop(0, 4, finish_group, 0)


def operator(features, leaf_in, mix_in, mix_out, leaf_out):
    hbm = pl.BlockSpec(memory_space=pltpu.HBM)
    dma = pltpu.SemaphoreType.DMA
    return pl.pallas_call(
        operator_kernel,
        out_shape=jax.ShapeDtypeStruct((2, 2, 2, 4, RANK, LANES), BF16),
        in_specs=[hbm] * 5,
        out_specs=hbm,
        scratch_shapes=[
            pltpu.VMEM((4, 2 * LEAF, 512), BF16),
            pltpu.VMEM((2 * LEAF, RANK), BF16),
            pltpu.VMEM((2, RANK, LEAF), BF16),
            pltpu.VMEM((16, LEVELS, RANK, 2 * RANK), BF16),
            pltpu.VMEM((2, 2, 2 * RANK, 2 * RANK), BF16),
            pltpu.VMEM((2, 8, 2 * RANK, 2 * RANK), BF16),
            pltpu.VMEM((LEVELS, 16, RANK, 2 * RANK), BF16),
            pltpu.VMEM((LEVELS, 8, 2 * RANK, 2 * RANK), BF16),
            pltpu.VMEM((16 * LEAF, RANK), BF16),
            pltpu.VMEM((16, RANK, 2 * RANK), BF16),
            pltpu.VMEM((2, 2, 2, 4, RANK, LANES), BF16),
            pltpu.VMEM((2, 4, 4, RANK, LANES), BF16),
            pltpu.VMEM((2, 16, RANK, LANES), BF16),
            pltpu.VMEM((2, 16, RANK, LANES), BF16),
            pltpu.VMEM((2, 16, RANK, LANES), BF16),
            pltpu.VMEM((2, 4, 4, RANK, LANES), BF16),
            dma((8,)), dma((8,)), dma((8,)), dma((10,)), dma((10,)),
            dma((6, 2, 16)), dma((6, 2)),
        ],
        compiler_params=pltpu.CompilerParams(
            collective_id=0, has_side_effects=True, vmem_limit_bytes=56 << 20
        ),
        name="operator",
    )(features, leaf_in, mix_in, mix_out, leaf_out)


def expand_kernel(rows_in, blocks_in, out, rows, blocks, wide, sems):
    row_loads, block_loads = [], []
    for leaf in range(2):
        half = pl.ds(leaf * LEAF, LEAF)
        row_loads.append(pltpu.make_async_copy(rows_in.at[half], rows.at[half], sems.at[8 + leaf]))
        row_loads[-1].start()
        for q in range(2):
            block_loads.append(
                pltpu.make_async_copy(
                    blocks_in.at[q, :, leaf], blocks.at[q, :, leaf], sems.at[10 + 2 * leaf + q]
                )
            )
            block_loads[-1].start()
    stores = []
    for leaf in range(2):
        here = pl.ds(leaf * LEAF, LEAF)
        row_loads[leaf].wait()
        for part in range(4):
            if part % 2 == 0:
                block_loads[2 * leaf + part // 2].wait()
            for i in range(2):
                q, side = part // 2, part % 2 * 2 + i
                columns = jnp.concatenate(
                    [blocks[q, 0, leaf, side], blocks[q, 1, leaf, side]], axis=1
                )
                wide[here, pl.ds(part * 512 + i * 256, 256)] = jnp.dot(
                    rows[here, :], columns, preferred_element_type=F32
                ).astype(BF16)
            tile = pl.ds(part * 512, 512)
            store = pltpu.make_async_copy(
                wide.at[here, tile], out.at[here, tile], sems.at[len(stores)]
            )
            store.start()
            stores.append(store)
    for store in stores:
        store.wait()


def expand(leaf_in, returned, columns):
    hbm = pl.BlockSpec(memory_space=pltpu.HBM)
    return pl.pallas_call(
        expand_kernel,
        out_shape=jax.ShapeDtypeStruct((2 * LEAF, columns), BF16),
        in_specs=[hbm, hbm],
        out_specs=hbm,
        scratch_shapes=[
            pltpu.VMEM((2 * LEAF, RANK), BF16),
            pltpu.VMEM(returned.shape, BF16),
            pltpu.VMEM((2 * LEAF, columns), BF16),
            pltpu.SemaphoreType.DMA((14,)),
        ],
        compiler_params=pltpu.CompilerParams(vmem_limit_bytes=58 << 20),
        name="expand",
    )(leaf_in, returned)


def body(features, leaf_in, mix_in, mix_out, leaf_out):
    returned = operator(features, leaf_in, mix_in, mix_out, leaf_out)
    return expand(leaf_in, returned, features.shape[1])


def solution(mesh):
    in_specs = (
        P(("col", "row"), None),
        P(("col", "row"), None),
        P(None, ("col", "row"), None, None),
        P(None, "col", None, None),
        P("col", None),
    )
    out_specs = P(("col", "row"), None)
    return jax.shard_map(body, mesh=mesh, in_specs=in_specs, out_specs=out_specs, check_vma=False)
```

```python
import jax
import jax.numpy as jnp
from jax import lax
from jax.experimental import pallas as pl
from jax.experimental.pallas import tpu as pltpu
from jax.sharding import PartitionSpec as P

LEAF = 1024
RANK = 128
LANES = 128
MESH = pl.DeviceIdType.MESH
F32 = jnp.float32
BF16 = jnp.bfloat16
LEVELS = 4


def pairs_of(bit):
    return [b for b in range(16) if not b >> bit & 1]


def pair_matrix(top, bottom):
    swapped = jnp.concatenate([bottom[:, RANK:], bottom[:, :RANK]], axis=1)
    return jnp.concatenate([top, swapped], axis=0)


def column(x, zl, k):
    return x * 4 + zl * 2 + k


def operator_kernel(
    features, leaf_in, mix_in, mix_out, leaf_out, returned,
    feat, basis, basis_t, win, near_t, far_t, wout, wout_t, lout, gram,
    coeffs, xz, xa, xb, xr, zr,
    load_sem, w_send, w_recv, sib_send, sib_recv, send_sem, recv_sem,
):
    col, row = lax.axis_index("col"), lax.axis_index("row")
    x, zl, k = col // 4, col // 2 % 2, col % 2
    zh, y = row // 4, row % 4
    x_hi, x_lo, y_hi, y_lo = x // 2, x % 2, y // 2, y % 2
    right, left = (x + 1) % 4, (x + 3) % 4

    feat_loads = [
        pltpu.make_async_copy(
            features.at[:, pl.ds(j * 512, 512)], feat.at[j], load_sem.at[j]
        )
        for j in range(4)
    ]
    basis_load = pltpu.make_async_copy(leaf_in, basis, load_sem.at[4])
    wout_load = pltpu.make_async_copy(mix_out, wout, load_sem.at[5])
    lout_load = pltpu.make_async_copy(leaf_out, lout, load_sem.at[6])
    own_load = pltpu.make_async_copy(mix_in.at[:, zl], win.at[col], load_sem.at[7])
    def relative(m):
        px = (x + m + 1) % 4
        pz = (zl + m + m // 4) % 2
        pk = (k + m // 2 + m // 8) % 2
        return px, pz, pk

    def spread_row(m):
        px, pz, pk = relative(m)
        py = (x_lo + px) % 2 * 2 + (x_hi + pk) % 2
        return column(px, pz, pk), k * 4 + py

    def gather_row(m):
        px = (y_lo + k) % 2 * 2 + (y_hi + x) % 2
        pz, py, ph = m % 2, m // 2 % 4, m // 8
        return column(px, pz, zh), ph * 4 + py, (ph * 4 + py) * 2 + pz

    barrier = pltpu.get_barrier_semaphore()

    def greet(m, carry):
        for c, r in (spread_row(m), gather_row(m)[:2]):
            pl.semaphore_signal(barrier, device_id={"col": c, "row": r}, device_id_type=MESH)
        return carry

    def near(m):
        pz, pk = (zl + m + 1) % 2, (k + m // 2 + 1) % 2
        return pz, pk, column(x, pz, pk)

    def across(m):
        px = (x + m + 1) % 4
        return px, column(px, zl, k)

    def greet_group(m, carry):
        for c in (near(m)[-1], across(m)[-1]):
            pl.semaphore_signal(barrier, device_id={"col": c, "row": row}, device_id_type=MESH)
        return carry

    for load in [basis_load, *feat_loads[:2]]:
        load.start()
    lax.fori_loop(0, 4, greet_group, 0)
    lax.fori_loop(0, 16, greet, 0, unroll=True)
    pl.semaphore_wait(barrier, 40)

    def ship(src, dst, send, recv, c, r):
        here = jnp.logical_and(c == col, r == row)

        @pl.when(here)
        def _():
            pltpu.make_async_copy(src, dst, recv).start()

        @pl.when(jnp.logical_not(here))
        def _():
            pltpu.make_async_remote_copy(
                src_ref=src, dst_ref=dst, send_sem=send, recv_sem=recv,
                device_id={"col": c, "row": r}, device_id_type=MESH,
            ).start()

    def drain(src, send, c, r):
        here = jnp.logical_and(c == col, r == row)

        @pl.when(jnp.logical_not(here))
        def _():
            pltpu.make_async_remote_copy(
                src_ref=src, dst_ref=src, send_sem=send, recv_sem=send,
                device_id={"col": c, "row": r}, device_id_type=MESH,
            ).wait_send()

    early, late = pl.ds(0, 2), pl.ds(2, 2)

    def weights_to(src, slot, levels, n, recv, c):
        copy = pltpu.make_async_remote_copy(
            src_ref=src, dst_ref=win.at[slot, levels], send_sem=w_send.at[n], recv_sem=recv,
            device_id={"col": c}, device_id_type=MESH,
        )
        copy.start()
        return copy

    def arrived(slot, levels, sem):
        block = win.at[slot, levels]
        pltpu.make_async_copy(block, block, sem).wait()

    siblings = []

    def to_sibling(src, slot, levels):
        n = len(siblings)
        copy = pltpu.make_async_remote_copy(
            src_ref=src, dst_ref=win.at[slot, levels],
            send_sem=sib_send.at[n], recv_sem=sib_recv.at[n],
            device_id={"col": column(x, zl, 1 - k)}, device_id_type=MESH,
        )
        copy.start()
        siblings.append(copy)

    partner = column(x, 1 - zl, k)
    gives = [
        weights_to(mix_in.at[late, 1 - zl], col, late, 0, w_recv.at[0], partner),
        weights_to(mix_in.at[late, zl], col, late, 1, w_recv.at[1 + zl], column(right, zl, k)),
        weights_to(mix_in.at[late, zl], col, late, 2, w_recv.at[3 + zl], column(left, zl, k)),
        weights_to(mix_in.at[early, 1 - zl], col, early, 7, w_recv.at[7], partner),
    ]
    to_sibling(mix_in.at[early, zl], col, early)
    for load in [*feat_loads[2:], own_load]:
        load.start()

    basis_load.wait()
    for leaf in range(2):
        basis_t[leaf] = basis[pl.ds(leaf * LEAF, LEAF), :].T

    def project(q):
        for j in range(2):
            feat_loads[2 * q + j].wait()
            for leaf in range(2):
                block = jnp.dot(
                    basis_t[leaf], feat[2 * q + j, pl.ds(leaf * LEAF, LEAF), :],
                    preferred_element_type=F32,
                ).astype(BF16)
                for i in range(4):
                    coeffs[q, i % 2, leaf, 2 * j + i // 2] = block[:, i * LANES : (i + 1) * LANES]

    def send_coeffs(q):
        def one(m, carry):
            pz, pk, to = near(m)
            ship(
                coeffs.at[q, pk, pz], xz.at[q, zl * 2 + k],
                send_sem.at[0, q, m], recv_sem.at[0, q], to, row,
            )
            return carry

        lax.fori_loop(0, 4, one, 0, unroll=True)

    project(0)
    send_coeffs(0)
    arrived(partner, late, w_recv.at[0])
    block = win.at[partner, late]
    gives += [
        weights_to(block, partner, late, 3, w_recv.at[2 - zl], column(right, zl, k)),
        weights_to(block, partner, late, 4, w_recv.at[4 - zl], column(left, zl, k)),
    ]
    project(1)
    send_coeffs(1)
    lout_load.start()
    wout_load.start()
    arrived(partner, early, w_recv.at[7])
    to_sibling(win.at[partner, early], partner, early)
    to_sibling(mix_in.at[late, zl], col, late)
    to_sibling(win.at[partner, late], partner, late)

    from_left = [column(left, z, k) for z in range(2)]
    from_right = [column(right, z, k) for z in range(2)]
    for slot, sem, n, c in (
        (from_right[0], 3, 5, column(left, zl, k)),
        (from_left[1], 2, 6, column(right, zl, k)),
    ):
        arrived(slot, late, w_recv.at[sem])
        gives.append(weights_to(win.at[slot, late], slot, late, n, w_recv.at[n], c))
        to_sibling(win.at[slot, late], slot, late)
    for slot, sem in ((from_left[0], 1), (from_right[1], 4)):
        arrived(slot, late, w_recv.at[sem])
        to_sibling(win.at[slot, late], slot, late)

    def received(buffer, phase, q):
        pltpu.make_async_copy(buffer.at[q], buffer.at[q], recv_sem.at[phase, q]).wait()

    def mix_near(buffer, q, level, matrix):
        for n, b in enumerate(b for b in range(4) if not b >> level & 1):
            p = b | 1 << level
            for i in (0, 2):
                stack = jnp.concatenate(
                    [
                        jnp.concatenate([buffer[q, c, i], buffer[q, c, i + 1]], axis=1)
                        for c in (b, p)
                    ],
                    axis=0,
                )
                mixed = jnp.dot(
                    matrix(level, n, b, p), stack, preferred_element_type=F32
                ).astype(BF16)
                for c, part in ((b, mixed[:RANK]), (p, mixed[RANK:])):
                    buffer[q, c, i] = part[:, :LANES]
                    buffer[q, c, i + 1] = part[:, LANES:]

    def near_matrix(level, n, b, p):
        return pair_matrix(win[x * 4 + b, level], win[x * 4 + p, level])

    own_load.wait()
    for copy in siblings[:2]:
        copy.wait_recv()

    def near_side(q, carry):
        received(xz, 0, q)
        for level in range(2):
            mix_near(xz, q, level, near_matrix)

        def one(m, c):
            px, to = across(m)
            ship(
                xz.at[q, :, px], xa.at[q, pl.ds(x * 4, 4)],
                send_sem.at[1, q, m], recv_sem.at[1, q], to, row,
            )
            return c

        lax.fori_loop(0, 4, one, 0, unroll=True)
        return carry

    near_side(0, 0)

    far = (x + 2) % 4
    for z in range(2):
        slot = column(far, z, k)
        arrived(slot, late, w_recv.at[5 + z])
        to_sibling(win.at[slot, late], slot, late)

    lout_load.wait()

    def gram_of(i, carry):
        rows = lout[pl.ds(i * LEAF, LEAF), :]
        product = lax.dot_general(rows, rows, (((0,), (0,)), ((), ())), preferred_element_type=F32)
        high = product.astype(BF16)
        low = (product - high.astype(F32)).astype(BF16)
        gram[i] = jnp.concatenate([high, low], axis=1)
        return carry

    lax.fori_loop(0, 16, gram_of, 0)
    near_side(1, 0)

    wout_load.wait()

    for level in range(LEVELS):
        for n, b in enumerate(pairs_of(level)):
            wout_t[level, n] = pair_matrix(wout[level, b], wout[level, b | 1 << level]).T

    for copy in siblings[2:]:
        copy.wait_recv()

    def mix(buffer, q, level, matrix):
        for n, b in enumerate(pairs_of(level)):
            p = b | 1 << level
            stack = jnp.concatenate([buffer[q, b], buffer[q, p]], axis=0)
            mixed = jnp.dot(matrix(level, n, b, p), stack, preferred_element_type=F32).astype(BF16)
            buffer[q, b] = mixed[:RANK]
            buffer[q, p] = mixed[RANK:]

    def forward_in(level, n, b, p):
        return pair_matrix(win[b, level], win[p, level])

    def forward_out(level, n, b, p):
        return pair_matrix(wout[level, b], wout[level, p])

    def backward_in(level, n, b, p):
        return far_t[level - 2, n]

    def backward_near(level, n, b, p):
        return near_t[level, n]

    def backward_out(level, n, b, p):
        return wout_t[level, n]

    def input_side(q, carry):
        received(xa, 1, q)
        for level in (2, 3):
            mix(xa, q, level, forward_in)

        def one(m, c):
            px, pz, pk = relative(m)
            to, r = spread_row(m)
            ship(
                xa.at[q, to], xb.at[q, row * 2 + zl],
                send_sem.at[2, q, m], recv_sem.at[2, q], to, r,
            )
            return c

        lax.fori_loop(0, 16, one, 0, unroll=True)
        return carry

    lax.fori_loop(0, 2, input_side, 0)

    for level in (2, 3):
        for n, b in enumerate(pairs_of(level)):
            far_t[level - 2, n] = pair_matrix(win[b, level], win[b | 1 << level, level]).T
    for level in range(2):
        for n, b in enumerate(b for b in range(4) if not b >> level & 1):
            near_t[level, n] = near_matrix(level, n, b, b | 1 << level).T

    def output_side(q, carry):
        received(xb, 2, q)
        for level in range(LEVELS):
            mix(xb, q, level, forward_out)
        for b in range(16):
            twice = jnp.concatenate([xb[q, b], xb[q, b]], axis=0)
            xb[q, b] = jnp.dot(gram[b], twice, preferred_element_type=F32).astype(BF16)
        for level in reversed(range(LEVELS)):
            mix(xb, q, level, backward_out)

        def one(m, c):
            to, r, b = gather_row(m)
            ship(
                xb.at[q, b], xr.at[q, col],
                send_sem.at[3, q, m], recv_sem.at[3, q], to, r,
            )
            return c

        lax.fori_loop(0, 16, one, 0, unroll=True)
        return carry

    lax.fori_loop(0, 2, output_side, 0)

    for copy in gives + siblings:
        copy.wait_send()

    def finish_spread(m, carry):
        for q in range(2):
            c, r = spread_row(m)
            drain(xa.at[q, c], send_sem.at[2, q, m], c, r)
        return carry

    lax.fori_loop(0, 16, finish_spread, 0)

    def finish_group(m, carry):
        for q in range(2):
            pz, pk, to = near(m)
            drain(coeffs.at[q, pk, pz], send_sem.at[0, q, m], to, row)
            px, to = across(m)
            drain(xz.at[q, :, px], send_sem.at[1, q, m], to, row)
        return carry

    lax.fori_loop(0, 4, finish_group, 0)

    def input_side_back(q, carry):
        received(xr, 3, q)
        for level in (3, 2):
            mix(xr, q, level, backward_in)

        def one(m, c):
            px, to = across(m)
            ship(
                xr.at[q, pl.ds(px * 4, 4)], zr.at[q, :, x],
                send_sem.at[4, q, m], recv_sem.at[4, q], to, row,
            )
            return c

        lax.fori_loop(0, 4, one, 0, unroll=True)
        return carry

    lax.fori_loop(0, 2, input_side_back, 0)

    def finish_gather(m, carry):
        for q in range(2):
            c, r, b = gather_row(m)
            drain(xb.at[q, b], send_sem.at[3, q, m], c, r)
        return carry

    lax.fori_loop(0, 16, finish_gather, 0)

    def near_side_back(q, carry):
        received(zr, 4, q)
        for level in (1, 0):
            mix_near(zr, q, level, backward_near)

        def one(m, c):
            pz, pk, to = near(m)
            ship(
                zr.at[q, pz * 2 + pk], returned.at[q, k, zl],
                send_sem.at[5, q, m], recv_sem.at[5, q], to, row,
            )
            return c

        lax.fori_loop(0, 4, one, 0, unroll=True)
        return carry

    lax.fori_loop(0, 2, near_side_back, 0)

    def finish_across(m, carry):
        for q in range(2):
            px, to = across(m)
            drain(xr.at[q, pl.ds(px * 4, 4)], send_sem.at[4, q, m], to, row)
        return carry

    lax.fori_loop(0, 4, finish_across, 0)

    for q in range(2):
        received(returned, 5, q)

    def finish_back(m, carry):
        for q in range(2):
            pz, pk, to = near(m)
            drain(zr.at[q, pz * 2 + pk], send_sem.at[5, q, m], to, row)
        return carry

    lax.fori_loop(0, 4, finish_back, 0)


def operator(features, leaf_in, mix_in, mix_out, leaf_out):
    hbm = pl.BlockSpec(memory_space=pltpu.HBM)
    dma = pltpu.SemaphoreType.DMA
    return pl.pallas_call(
        operator_kernel,
        out_shape=jax.ShapeDtypeStruct((2, 2, 2, 4, RANK, LANES), BF16),
        in_specs=[hbm] * 5,
        out_specs=hbm,
        scratch_shapes=[
            pltpu.VMEM((4, 2 * LEAF, 512), BF16),
            pltpu.VMEM((2 * LEAF, RANK), BF16),
            pltpu.VMEM((2, RANK, LEAF), BF16),
            pltpu.VMEM((16, LEVELS, RANK, 2 * RANK), BF16),
            pltpu.VMEM((2, 2, 2 * RANK, 2 * RANK), BF16),
            pltpu.VMEM((2, 8, 2 * RANK, 2 * RANK), BF16),
            pltpu.VMEM((LEVELS, 16, RANK, 2 * RANK), BF16),
            pltpu.VMEM((LEVELS, 8, 2 * RANK, 2 * RANK), BF16),
            pltpu.VMEM((16 * LEAF, RANK), BF16),
            pltpu.VMEM((16, RANK, 2 * RANK), BF16),
            pltpu.VMEM((2, 2, 2, 4, RANK, LANES), BF16),
            pltpu.VMEM((2, 4, 4, RANK, LANES), BF16),
            pltpu.VMEM((2, 16, RANK, LANES), BF16),
            pltpu.VMEM((2, 16, RANK, LANES), BF16),
            pltpu.VMEM((2, 16, RANK, LANES), BF16),
            pltpu.VMEM((2, 4, 4, RANK, LANES), BF16),
            dma((8,)), dma((8,)), dma((8,)), dma((10,)), dma((10,)),
            dma((6, 2, 16)), dma((6, 2)),
        ],
        compiler_params=pltpu.CompilerParams(
            collective_id=0, has_side_effects=True, vmem_limit_bytes=56 << 20
        ),
        name="operator",
    )(features, leaf_in, mix_in, mix_out, leaf_out)


def expand_kernel(rows_in, blocks_in, out, rows, blocks, wide, sems):
    row_loads, block_loads = [], []
    for leaf in range(2):
        half = pl.ds(leaf * LEAF, LEAF)
        row_loads.append(pltpu.make_async_copy(rows_in.at[half], rows.at[half], sems.at[8 + leaf]))
        row_loads[-1].start()
        for q in range(2):
            block_loads.append(
                pltpu.make_async_copy(
                    blocks_in.at[q, :, leaf], blocks.at[q, :, leaf], sems.at[10 + 2 * leaf + q]
                )
            )
            block_loads[-1].start()
    stores = []
    for leaf in range(2):
        here = pl.ds(leaf * LEAF, LEAF)
        row_loads[leaf].wait()
        for part in range(4):
            if part % 2 == 0:
                block_loads[2 * leaf + part // 2].wait()
            for i in range(2):
                q, side = part // 2, part % 2 * 2 + i
                columns = jnp.concatenate(
                    [blocks[q, 0, leaf, side], blocks[q, 1, leaf, side]], axis=1
                )
                wide[here, pl.ds(part * 512 + i * 256, 256)] = jnp.dot(
                    rows[here, :], columns, preferred_element_type=F32
                ).astype(BF16)
            tile = pl.ds(part * 512, 512)
            store = pltpu.make_async_copy(
                wide.at[here, tile], out.at[here, tile], sems.at[len(stores)]
            )
            store.start()
            stores.append(store)
    for store in stores:
        store.wait()


def expand(leaf_in, returned, columns):
    hbm = pl.BlockSpec(memory_space=pltpu.HBM)
    return pl.pallas_call(
        expand_kernel,
        out_shape=jax.ShapeDtypeStruct((2 * LEAF, columns), BF16),
        in_specs=[hbm, hbm],
        out_specs=hbm,
        scratch_shapes=[
            pltpu.VMEM((2 * LEAF, RANK), BF16),
            pltpu.VMEM(returned.shape, BF16),
            pltpu.VMEM((2 * LEAF, columns), BF16),
            pltpu.SemaphoreType.DMA((14,)),
        ],
        compiler_params=pltpu.CompilerParams(vmem_limit_bytes=58 << 20),
        name="expand",
    )(leaf_in, returned)


def body(features, leaf_in, mix_in, mix_out, leaf_out):
    returned = operator(features, leaf_in, mix_in, mix_out, leaf_out)
    return expand(leaf_in, returned, features.shape[1])


def solution(mesh):
    in_specs = (
        P(("col", "row"), None),
        P(("col", "row"), None),
        P(None, ("col", "row"), None, None),
        P(None, "col", None, None),
        P("col", None),
    )
    out_specs = P(("col", "row"), None)
    return jax.shard_map(body, mesh=mesh, in_specs=in_specs, out_specs=out_specs, check_vma=False)
```

```python
import jax
import jax.numpy as jnp
from jax import lax
from jax.experimental import pallas as pl
from jax.experimental.pallas import tpu as pltpu
from jax.sharding import PartitionSpec as P

LEAF = 1024
RANK = 128
LANES = 128
MESH = pl.DeviceIdType.MESH
F32 = jnp.float32
BF16 = jnp.bfloat16
LEVELS = 4


def pairs_of(bit):
    return [b for b in range(16) if not b >> bit & 1]


def pair_matrix(top, bottom):
    swapped = jnp.concatenate([bottom[:, RANK:], bottom[:, :RANK]], axis=1)
    return jnp.concatenate([top, swapped], axis=0)


def column(x, zl, k):
    return x * 4 + zl * 2 + k


def operator_kernel(
    features, leaf_in, mix_in, mix_out, leaf_out, returned,
    feat, basis, basis_t, win, near_t, far_t, wout, wout_t, lout, gram,
    coeffs, xz, xa, xb, xr, zr,
    load_sem, w_send, w_recv, sib_send, sib_recv, send_sem, recv_sem,
):
    col, row = lax.axis_index("col"), lax.axis_index("row")
    x, zl, k = col // 4, col // 2 % 2, col % 2
    zh, y = row // 4, row % 4
    x_hi, x_lo, y_hi, y_lo = x // 2, x % 2, y // 2, y % 2
    right, left = (x + 1) % 4, (x + 3) % 4

    feat_loads = [
        pltpu.make_async_copy(
            features.at[:, pl.ds(j * 512, 512)], feat.at[j], load_sem.at[j]
        )
        for j in range(4)
    ]
    basis_load = pltpu.make_async_copy(leaf_in, basis, load_sem.at[4])
    wout_load = pltpu.make_async_copy(mix_out, wout, load_sem.at[5])
    lout_load = pltpu.make_async_copy(leaf_out, lout, load_sem.at[6])
    own_load = pltpu.make_async_copy(mix_in.at[:, zl], win.at[col], load_sem.at[7])
    def relative(m):
        px = (x + m + 1) % 4
        pz = (zl + m + m // 4) % 2
        pk = (k + m // 2 + m // 8) % 2
        return px, pz, pk

    def spread_row(m):
        px, pz, pk = relative(m)
        py = (x_lo + px) % 2 * 2 + (x_hi + pk) % 2
        return column(px, pz, pk), k * 4 + py

    def gather_row(m):
        px = (y_lo + k) % 2 * 2 + (y_hi + x) % 2
        pz, py, ph = m % 2, m // 2 % 4, m // 8
        return column(px, pz, zh), ph * 4 + py, (ph * 4 + py) * 2 + pz

    barrier = pltpu.get_barrier_semaphore()

    def greet(m, carry):
        for c, r in (spread_row(m), gather_row(m)[:2]):
            pl.semaphore_signal(barrier, device_id={"col": c, "row": r}, device_id_type=MESH)
        return carry

    def near(m):
        pz, pk = (zl + m + 1) % 2, (k + m // 2 + 1) % 2
        return pz, pk, column(x, pz, pk)

    def across(m):
        px = (x + m + 1) % 4
        return px, column(px, zl, k)

    def greet_group(m, carry):
        for c in (near(m)[-1], across(m)[-1]):
            pl.semaphore_signal(barrier, device_id={"col": c, "row": row}, device_id_type=MESH)
        return carry

    for load in [basis_load, *feat_loads[:2]]:
        load.start()
    lax.fori_loop(0, 4, greet_group, 0)
    lax.fori_loop(0, 16, greet, 0, unroll=True)
    pl.semaphore_wait(barrier, 40)

    def ship(src, dst, send, recv, c, r):
        here = jnp.logical_and(c == col, r == row)

        @pl.when(here)
        def _():
            pltpu.make_async_copy(src, dst, recv).start()

        @pl.when(jnp.logical_not(here))
        def _():
            pltpu.make_async_remote_copy(
                src_ref=src, dst_ref=dst, send_sem=send, recv_sem=recv,
                device_id={"col": c, "row": r}, device_id_type=MESH,
            ).start()

    def drain(src, send, c, r):
        here = jnp.logical_and(c == col, r == row)

        @pl.when(jnp.logical_not(here))
        def _():
            pltpu.make_async_remote_copy(
                src_ref=src, dst_ref=src, send_sem=send, recv_sem=send,
                device_id={"col": c, "row": r}, device_id_type=MESH,
            ).wait_send()

    early, late = pl.ds(0, 2), pl.ds(2, 2)

    def weights_to(src, slot, levels, n, recv, c):
        copy = pltpu.make_async_remote_copy(
            src_ref=src, dst_ref=win.at[slot, levels], send_sem=w_send.at[n], recv_sem=recv,
            device_id={"col": c}, device_id_type=MESH,
        )
        copy.start()
        return copy

    def arrived(slot, levels, sem):
        block = win.at[slot, levels]
        pltpu.make_async_copy(block, block, sem).wait()

    siblings = []

    def to_sibling(src, slot, levels):
        n = len(siblings)
        copy = pltpu.make_async_remote_copy(
            src_ref=src, dst_ref=win.at[slot, levels],
            send_sem=sib_send.at[n], recv_sem=sib_recv.at[n],
            device_id={"col": column(x, zl, 1 - k)}, device_id_type=MESH,
        )
        copy.start()
        siblings.append(copy)

    partner = column(x, 1 - zl, k)
    gives = [
        weights_to(mix_in.at[late, 1 - zl], col, late, 0, w_recv.at[0], partner),
        weights_to(mix_in.at[late, zl], col, late, 1, w_recv.at[1 + zl], column(right, zl, k)),
        weights_to(mix_in.at[late, zl], col, late, 2, w_recv.at[3 + zl], column(left, zl, k)),
        weights_to(mix_in.at[early, 1 - zl], col, early, 7, w_recv.at[7], partner),
    ]
    to_sibling(mix_in.at[early, zl], col, early)
    for load in [*feat_loads[2:], own_load]:
        load.start()

    basis_load.wait()
    for leaf in range(2):
        basis_t[leaf] = basis[pl.ds(leaf * LEAF, LEAF), :].T

    def project(q):
        for j in range(2):
            feat_loads[2 * q + j].wait()
            for leaf in range(2):
                block = jnp.dot(
                    basis_t[leaf], feat[2 * q + j, pl.ds(leaf * LEAF, LEAF), :],
                    preferred_element_type=F32,
                ).astype(BF16)
                for i in range(4):
                    coeffs[q, i % 2, leaf, 2 * j + i // 2] = block[:, i * LANES : (i + 1) * LANES]

    def send_coeffs(q):
        def one(m, carry):
            pz, pk, to = near(m)
            ship(
                coeffs.at[q, pk, pz], xz.at[q, zl * 2 + k],
                send_sem.at[0, q, m], recv_sem.at[0, q], to, row,
            )
            return carry

        lax.fori_loop(0, 4, one, 0, unroll=True)

    project(0)
    send_coeffs(0)
    arrived(partner, late, w_recv.at[0])
    block = win.at[partner, late]
    gives += [
        weights_to(block, partner, late, 3, w_recv.at[2 - zl], column(right, zl, k)),
        weights_to(block, partner, late, 4, w_recv.at[4 - zl], column(left, zl, k)),
    ]
    project(1)
    send_coeffs(1)
    lout_load.start()
    wout_load.start()
    arrived(partner, early, w_recv.at[7])
    to_sibling(win.at[partner, early], partner, early)
    to_sibling(mix_in.at[late, zl], col, late)
    to_sibling(win.at[partner, late], partner, late)

    from_left = [column(left, z, k) for z in range(2)]
    from_right = [column(right, z, k) for z in range(2)]
    for slot, sem, n, c in (
        (from_right[0], 3, 5, column(left, zl, k)),
        (from_left[1], 2, 6, column(right, zl, k)),
    ):
        arrived(slot, late, w_recv.at[sem])
        gives.append(weights_to(win.at[slot, late], slot, late, n, w_recv.at[n], c))
        to_sibling(win.at[slot, late], slot, late)
    for slot, sem in ((from_left[0], 1), (from_right[1], 4)):
        arrived(slot, late, w_recv.at[sem])
        to_sibling(win.at[slot, late], slot, late)

    def received(buffer, phase, q):
        pltpu.make_async_copy(buffer.at[q], buffer.at[q], recv_sem.at[phase, q]).wait()

    def mix_near(buffer, q, level, matrix):
        for n, b in enumerate(b for b in range(4) if not b >> level & 1):
            p = b | 1 << level
            for i in (0, 2):
                stack = jnp.concatenate(
                    [
                        jnp.concatenate([buffer[q, c, i], buffer[q, c, i + 1]], axis=1)
                        for c in (b, p)
                    ],
                    axis=0,
                )
                mixed = jnp.dot(
                    matrix(level, n, b, p), stack, preferred_element_type=F32
                ).astype(BF16)
                for c, part in ((b, mixed[:RANK]), (p, mixed[RANK:])):
                    buffer[q, c, i] = part[:, :LANES]
                    buffer[q, c, i + 1] = part[:, LANES:]

    def near_matrix(level, n, b, p):
        return pair_matrix(win[x * 4 + b, level], win[x * 4 + p, level])

    own_load.wait()
    for copy in siblings[:2]:
        copy.wait_recv()

    def near_side(q, carry):
        received(xz, 0, q)
        for level in range(2):
            mix_near(xz, q, level, near_matrix)

        def one(m, c):
            px, to = across(m)
            ship(
                xz.at[q, :, px], xa.at[q, pl.ds(x * 4, 4)],
                send_sem.at[1, q, m], recv_sem.at[1, q], to, row,
            )
            return c

        lax.fori_loop(0, 4, one, 0, unroll=True)
        return carry

    near_side(0, 0)

    far = (x + 2) % 4
    for z in range(2):
        slot = column(far, z, k)
        arrived(slot, late, w_recv.at[5 + z])
        to_sibling(win.at[slot, late], slot, late)

    lout_load.wait()

    def gram_of(i, carry):
        rows = lout[pl.ds(i * LEAF, LEAF), :]
        product = lax.dot_general(rows, rows, (((0,), (0,)), ((), ())), preferred_element_type=F32)
        high = product.astype(BF16)
        low = (product - high.astype(F32)).astype(BF16)
        gram[i] = jnp.concatenate([high, low], axis=1)
        return carry

    lax.fori_loop(0, 16, gram_of, 0)
    near_side(1, 0)

    wout_load.wait()
    for copy in siblings[2:]:
        copy.wait_recv()

    def mix(buffer, q, level, matrix):
        for n, b in enumerate(pairs_of(level)):
            p = b | 1 << level
            stack = jnp.concatenate([buffer[q, b], buffer[q, p]], axis=0)
            mixed = jnp.dot(matrix(level, n, b, p), stack, preferred_element_type=F32).astype(BF16)
            buffer[q, b] = mixed[:RANK]
            buffer[q, p] = mixed[RANK:]

    def forward_in(level, n, b, p):
        return pair_matrix(win[b, level], win[p, level])

    def forward_out(level, n, b, p):
        return pair_matrix(wout[level, b], wout[level, p])

    def backward_in(level, n, b, p):
        return far_t[level - 2, n]

    def backward_near(level, n, b, p):
        return near_t[level, n]

    def backward_out(level, n, b, p):
        return wout_t[level, n]

    def input_side(q, carry):
        received(xa, 1, q)
        for level in (2, 3):
            mix(xa, q, level, forward_in)

        def one(m, c):
            px, pz, pk = relative(m)
            to, r = spread_row(m)
            ship(
                xa.at[q, to], xb.at[q, row * 2 + zl],
                send_sem.at[2, q, m], recv_sem.at[2, q], to, r,
            )
            return c

        lax.fori_loop(0, 16, one, 0, unroll=True)
        return carry

    lax.fori_loop(0, 2, input_side, 0)

    for level in (2, 3):
        for n, b in enumerate(pairs_of(level)):
            far_t[level - 2, n] = pair_matrix(win[b, level], win[b | 1 << level, level]).T
    for level in range(2):
        for n, b in enumerate(b for b in range(4) if not b >> level & 1):
            near_t[level, n] = near_matrix(level, n, b, b | 1 << level).T

    for level in range(LEVELS):
        for n, b in enumerate(pairs_of(level)):
            wout_t[level, n] = pair_matrix(wout[level, b], wout[level, b | 1 << level]).T

    def output_side(q, carry):
        received(xb, 2, q)
        for level in range(LEVELS):
            mix(xb, q, level, forward_out)
        for b in range(16):
            twice = jnp.concatenate([xb[q, b], xb[q, b]], axis=0)
            xb[q, b] = jnp.dot(gram[b], twice, preferred_element_type=F32).astype(BF16)
        for level in reversed(range(LEVELS)):
            mix(xb, q, level, backward_out)

        def one(m, c):
            to, r, b = gather_row(m)
            ship(
                xb.at[q, b], xr.at[q, col],
                send_sem.at[3, q, m], recv_sem.at[3, q], to, r,
            )
            return c

        lax.fori_loop(0, 16, one, 0, unroll=True)
        return carry

    lax.fori_loop(0, 2, output_side, 0)

    for copy in gives + siblings:
        copy.wait_send()

    def finish_spread(m, carry):
        for q in range(2):
            c, r = spread_row(m)
            drain(xa.at[q, c], send_sem.at[2, q, m], c, r)
        return carry

    lax.fori_loop(0, 16, finish_spread, 0)

    def finish_group(m, carry):
        for q in range(2):
            pz, pk, to = near(m)
            drain(coeffs.at[q, pk, pz], send_sem.at[0, q, m], to, row)
            px, to = across(m)
            drain(xz.at[q, :, px], send_sem.at[1, q, m], to, row)
        return carry

    lax.fori_loop(0, 4, finish_group, 0)

    def input_side_back(q, carry):
        received(xr, 3, q)
        for level in (3, 2):
            mix(xr, q, level, backward_in)

        def one(m, c):
            px, to = across(m)
            ship(
                xr.at[q, pl.ds(px * 4, 4)], zr.at[q, :, x],
                send_sem.at[4, q, m], recv_sem.at[4, q], to, row,
            )
            return c

        lax.fori_loop(0, 4, one, 0, unroll=True)
        return carry

    lax.fori_loop(0, 2, input_side_back, 0)

    def finish_gather(m, carry):
        for q in range(2):
            c, r, b = gather_row(m)
            drain(xb.at[q, b], send_sem.at[3, q, m], c, r)
        return carry

    lax.fori_loop(0, 16, finish_gather, 0)

    def near_side_back(q, carry):
        received(zr, 4, q)
        for level in (1, 0):
            mix_near(zr, q, level, backward_near)

        def one(m, c):
            pz, pk, to = near(m)
            ship(
                zr.at[q, pz * 2 + pk], returned.at[q, k, zl],
                send_sem.at[5, q, m], recv_sem.at[5, q], to, row,
            )
            return c

        lax.fori_loop(0, 4, one, 0, unroll=True)
        return carry

    lax.fori_loop(0, 2, near_side_back, 0)

    def finish_across(m, carry):
        for q in range(2):
            px, to = across(m)
            drain(xr.at[q, pl.ds(px * 4, 4)], send_sem.at[4, q, m], to, row)
        return carry

    lax.fori_loop(0, 4, finish_across, 0)

    for q in range(2):
        received(returned, 5, q)

    def finish_back(m, carry):
        for q in range(2):
            pz, pk, to = near(m)
            drain(zr.at[q, pz * 2 + pk], send_sem.at[5, q, m], to, row)
        return carry

    lax.fori_loop(0, 4, finish_back, 0)


def operator(features, leaf_in, mix_in, mix_out, leaf_out):
    hbm = pl.BlockSpec(memory_space=pltpu.HBM)
    dma = pltpu.SemaphoreType.DMA
    return pl.pallas_call(
        operator_kernel,
        out_shape=jax.ShapeDtypeStruct((2, 2, 2, 4, RANK, LANES), BF16),
        in_specs=[hbm] * 5,
        out_specs=hbm,
        scratch_shapes=[
            pltpu.VMEM((4, 2 * LEAF, 512), BF16),
            pltpu.VMEM((2 * LEAF, RANK), BF16),
            pltpu.VMEM((2, RANK, LEAF), BF16),
            pltpu.VMEM((16, LEVELS, RANK, 2 * RANK), BF16),
            pltpu.VMEM((2, 2, 2 * RANK, 2 * RANK), BF16),
            pltpu.VMEM((2, 8, 2 * RANK, 2 * RANK), BF16),
            pltpu.VMEM((LEVELS, 16, RANK, 2 * RANK), BF16),
            pltpu.VMEM((LEVELS, 8, 2 * RANK, 2 * RANK), BF16),
            pltpu.VMEM((16 * LEAF, RANK), BF16),
            pltpu.VMEM((16, RANK, 2 * RANK), BF16),
            pltpu.VMEM((2, 2, 2, 4, RANK, LANES), BF16),
            pltpu.VMEM((2, 4, 4, RANK, LANES), BF16),
            pltpu.VMEM((2, 16, RANK, LANES), BF16),
            pltpu.VMEM((2, 16, RANK, LANES), BF16),
            pltpu.VMEM((2, 16, RANK, LANES), BF16),
            pltpu.VMEM((2, 4, 4, RANK, LANES), BF16),
            dma((8,)), dma((8,)), dma((8,)), dma((10,)), dma((10,)),
            dma((6, 2, 16)), dma((6, 2)),
        ],
        compiler_params=pltpu.CompilerParams(
            collective_id=0, has_side_effects=True, vmem_limit_bytes=56 << 20
        ),
        name="operator",
    )(features, leaf_in, mix_in, mix_out, leaf_out)


def expand_kernel(rows_in, blocks_in, out, rows, blocks, wide, sems):
    row_loads, block_loads = [], []
    for leaf in range(2):
        half = pl.ds(leaf * LEAF, LEAF)
        row_loads.append(pltpu.make_async_copy(rows_in.at[half], rows.at[half], sems.at[8 + leaf]))
        row_loads[-1].start()
        for q in range(2):
            block_loads.append(
                pltpu.make_async_copy(
                    blocks_in.at[q, :, leaf], blocks.at[q, :, leaf], sems.at[10 + 2 * leaf + q]
                )
            )
            block_loads[-1].start()
    stores = []
    for leaf in range(2):
        here = pl.ds(leaf * LEAF, LEAF)
        row_loads[leaf].wait()
        for part in range(4):
            if part % 2 == 0:
                block_loads[2 * leaf + part // 2].wait()
            for i in range(2):
                q, side = part // 2, part % 2 * 2 + i
                columns = jnp.concatenate(
                    [blocks[q, 0, leaf, side], blocks[q, 1, leaf, side]], axis=1
                )
                wide[here, pl.ds(part * 512 + i * 256, 256)] = jnp.dot(
                    rows[here, :], columns, preferred_element_type=F32
                ).astype(BF16)
            tile = pl.ds(part * 512, 512)
            store = pltpu.make_async_copy(
                wide.at[here, tile], out.at[here, tile], sems.at[len(stores)]
            )
            store.start()
            stores.append(store)
    for store in stores:
        store.wait()


def expand(leaf_in, returned, columns):
    hbm = pl.BlockSpec(memory_space=pltpu.HBM)
    return pl.pallas_call(
        expand_kernel,
        out_shape=jax.ShapeDtypeStruct((2 * LEAF, columns), BF16),
        in_specs=[hbm, hbm],
        out_specs=hbm,
        scratch_shapes=[
            pltpu.VMEM((2 * LEAF, RANK), BF16),
            pltpu.VMEM(returned.shape, BF16),
            pltpu.VMEM((2 * LEAF, columns), BF16),
            pltpu.SemaphoreType.DMA((14,)),
        ],
        compiler_params=pltpu.CompilerParams(vmem_limit_bytes=58 << 20),
        name="expand",
    )(leaf_in, returned)


def body(features, leaf_in, mix_in, mix_out, leaf_out):
    returned = operator(features, leaf_in, mix_in, mix_out, leaf_out)
    return expand(leaf_in, returned, features.shape[1])


def solution(mesh):
    in_specs = (
        P(("col", "row"), None),
        P(("col", "row"), None),
        P(None, ("col", "row"), None, None),
        P(None, "col", None, None),
        P("col", None),
    )
    out_specs = P(("col", "row"), None)
    return jax.shard_map(body, mesh=mesh, in_specs=in_specs, out_specs=out_specs, check_vma=False)
```
